32 devices in a mesh: seq: 8 (over z, core), head: 4 (over y, x).
Axes of the slice: x: 2, y: 2, z: 4, core: 2. Of those that a mesh axis runs over, the one named last changes fastest.
Arguments:
- inputs: float32 [8192, 5120], P(('seq', 'head')), may hold values from -6 to 6
- log_decay: float32 [8192, 80], P(('seq', 'head')), may hold values from -1 to 0
- input_map: float32 [8192, 128], P(('seq', 'head')), may hold values from -0.31533617 to 0.31533617
- output_map: float32 [8192, 128], P(('seq', 'head')), may hold values from -0.31533617 to 0.31533617
- skip_gain: float32 [80], replicated, may hold values from 0.5 to 2
Outputs:
- outputs: float32 [8192, 5120], P(('seq', 'head'))
The draws below stay inside these ranges and needn't reach their ends.
All inputs are finite; a program needn't handle non-finite values.
Results may differ from the reference program's by a relative error of at most 0.0001.
Values sent between devices are 32-bit elements; how exact they have to be, the bound alone decides.
A program may use at most 128 MiB of HBM per device.

```python
import math
from functools import partial
import jax
import jax.numpy as jnp
from jax import lax

HEADS = 80
HEAD_DIM = 64
STATE = 128
BLOCK = 128
TOK_DEV = 256
TOKEN_TOTAL = 8192


def draw_log_decay(key, part):
    fast_share = 0.2
    middle_share = 0.3
    class_key = jax.random.fold_in(key, 11)
    fast_rate_key = jax.random.fold_in(key, 12)
    slow_rate_key = jax.random.fold_in(key, 13)
    block_key = jax.random.fold_in(key, 14)
    jitter_key = jax.random.fold_in(key, 15)
    spike_random_key = jax.random.fold_in(key, 16)
    height_random_key = jax.random.fold_in(key, 17)
    middle_rate_key = jax.random.fold_in(key, 18)
    pick = jax.random.uniform(class_key, (HEADS,), jnp.float32)
    is_fast = pick < fast_share
    is_middle = jnp.logical_and(pick >= fast_share, pick < fast_share + middle_share)
    fast_rates = jnp.exp(jax.random.uniform(fast_rate_key, (HEADS,), jnp.float32, math.log(1.0 / 50.0), math.log(1.0 / 30.0)))
    middle_rates = jnp.exp(jax.random.uniform(middle_rate_key, (HEADS,), jnp.float32, math.log(0.0001), math.log(0.003)))
    slow_rates = jnp.exp(jax.random.uniform(slow_rate_key, (HEADS,), jnp.float32, math.log(0.05), math.log(0.35))) / TOKEN_TOTAL
    rates = jnp.where(is_fast, fast_rates, jnp.where(is_middle, middle_rates, slow_rates))
    block_scale = jnp.exp(jax.random.uniform(block_key, (TOKEN_TOTAL // TOK_DEV,), jnp.float32, math.log(0.6), math.log(1.6)))
    block_scale = jnp.repeat(block_scale, TOK_DEV)[:, None]
    jitter = jax.random.uniform(jitter_key, (TOKEN_TOTAL, HEADS), jnp.float32, 0.7, 1.3)
    value_entries = -rates[None, :] * block_scale * jitter
    spike_positions = jax.random.randint(spike_random_key, (2,), 0, TOKEN_TOTAL)
    spike_height = jnp.log(jax.random.uniform(height_random_key, (2,), jnp.float32, 0.5, 0.8))
    spike_hits = (jnp.arange(TOKEN_TOTAL)[:, None] == spike_positions[None, :]).astype(jnp.float32)
    value_entries = value_entries + jnp.sum(spike_hits * spike_height[None, :], axis=1)[:, None]
    return value_entries.astype(jnp.float32)


def level_of(own_key, dims, cuts, smallest, top_value):
    gain = 1.0
    for axis_at, parts in cuts:
        draws = jax.random.uniform(jax.random.fold_in(jax.random.fold_in(own_key, 6), axis_at), (parts,), jnp.float32, smallest / len(cuts), top_value / len(cuts))
        gain = gain * jnp.repeat(jnp.exp(draws), dims[axis_at] // parts).reshape((-1,) + (1,) * (len(dims) - 1 - axis_at))
    return gain


def gaussian(stream_key, dims, scale, limit, cuts=(), held_as=jnp.bfloat16):
    array = jax.random.normal(stream_key, dims, jnp.float32) * scale
    if len(cuts) > 0:
        array = level_of(stream_key, dims, cuts, -0.22, 0.18) * array
    return jnp.clip(array, min=-limit, max=limit).astype(held_as)


def setup_inputs(seed: int = 0) -> dict:
    keys = jax.random.split(jax.random.key(seed), 6)
    return {
        "inputs": gaussian(keys[0], (TOKEN_TOTAL, HEADS * HEAD_DIM), 1.0, 6.0, ((0, 32),), jnp.float32),
        "log_decay": draw_log_decay(jax.random.fold_in(keys[5], 71), 0),
        "input_map": gaussian(keys[2], (TOKEN_TOTAL, STATE), ((STATE * 1024) ** -0.25), 0.31533617, ((0, 32),), jnp.float32),
        "output_map": gaussian(keys[3], (TOKEN_TOTAL, STATE), ((STATE * 1024) ** -0.25), 0.31533617, ((0, 32),), jnp.float32),
        "skip_gain": jnp.clip(jnp.exp(jax.random.uniform(keys[4], (HEADS,), jnp.float32, math.log(0.5), math.log(2.0))), 0.5, 2.0),
    }


PRECISE = lax.Precision.HIGHEST


def block_pass(loop_carry, pieces, head_dim):
    memory, summed = loop_carry
    x_block, d_block, b_block, c_block = pieces
    length = d_block.shape[0]
    head_count = d_block.shape[1]
    running = jnp.cumsum(d_block, axis=0)
    positions = jnp.arange(length)
    causal = positions[:, None] >= positions[None, :]
    spread = running.T[:, :, None] - running.T[:, None, :]
    decays = jnp.where(causal[None], jnp.exp(jnp.minimum(spread, 0.0)), 0.0)
    scores = jnp.dot(c_block, b_block.T, precision=PRECISE)
    weighted = scores[None] * decays
    per_head = x_block.reshape(length, head_count, head_dim)
    within = jnp.einsum("hij,jhp->ihp", weighted, per_head, precision=PRECISE).reshape(length, head_count * head_dim)
    growth = jnp.repeat(jnp.exp(running), head_dim, axis=1)
    carried = jnp.dot(c_block, memory, precision=PRECISE) * growth
    closing = running[-1]
    remains = jnp.repeat(jnp.exp(closing[None, :] - running), head_dim, axis=1)
    memory = jnp.repeat(jnp.exp(closing), head_dim)[None, :] * memory + jnp.dot(b_block.T, x_block * remains, precision=PRECISE)
    prefix = running + summed[None, :]
    return (memory, summed + closing), (within + carried, prefix)


def scan_blocks(inputs, log_decay, input_map, output_map, memory, head_dim):
    token_count = inputs.shape[0]
    blocks = token_count // BLOCK
    pieces = (inputs.reshape(blocks, BLOCK, -1), log_decay.reshape(blocks, BLOCK, -1),
              input_map.reshape(blocks, BLOCK, -1), output_map.reshape(blocks, BLOCK, -1))
    start = jnp.zeros((log_decay.shape[1],), jnp.float32)
    (memory, summed), (results, prefix) = lax.scan(partial(block_pass, head_dim=head_dim), (memory, start), pieces)
    return results.reshape(token_count, -1), prefix.reshape(token_count, -1), memory, summed


def reference(inputs, log_decay, input_map, output_map, skip_gain):
    memory = jnp.zeros((STATE, HEADS * HEAD_DIM), jnp.float32)
    results, prefix, memory, summed = scan_blocks(inputs, log_decay, input_map, output_map, memory, HEAD_DIM)
    return results + inputs * jnp.repeat(skip_gain, HEAD_DIM)[None, :]
```

```python
import functools

import jax
import jax.numpy as jnp
from jax import lax
from jax.experimental import pallas as pl
from jax.experimental.pallas import tpu as pltpu
from jax.sharding import PartitionSpec as P

BLOCK = 128
LANES = 128
PRECISE = lax.Precision.HIGHEST
MESH = pl.DeviceIdType.MESH
F32 = jnp.float32
BF16 = jnp.bfloat16


def split2(value):
    high = value.astype(BF16)
    return high, (value - high.astype(F32)).astype(BF16)


def split3(value):
    high = value.astype(BF16)
    rest = value - high.astype(F32)
    middle = rest.astype(BF16)
    return high, middle, (rest - middle.astype(F32)).astype(BF16)


def dot(a, b):
    return jnp.dot(a, b, preferred_element_type=F32)


def dot3(a_high, a_low, b):
    b_high, b_low = split2(b)
    return dot(a_high, b_high) + (dot(a_high, b_low) + dot(a_low, b_high))


def piece_plan(width, groups):
    units = width // LANES
    per_owner = -(-units // groups)
    wide = 2 if units == per_owner * groups and per_owner % 2 == 0 else 1
    return per_owner // wide, wide * LANES


def kernel(
    groups, shards, chunks, piece, head_dim,
    x_hbm, d_ref, b_ref, c_ref, gain_ref, out_hbm,
    x_s, out_s, go_s, m0_s, ms_s, r_s, ps_s, pr_s, hin_s, hout_s, bef_s, a_s, rows_s,
    l_hi, l_lo, cm_hi, cm_lo, gi_hi, gi_lo, gx_hi, gx_lo, row_a, row_b, row_c, tot_s, totr_s,
    x_sem, o_sem, ms_send, ms_recv, ps_send, ps_recv, h_send, h_recv, t_send, t_recv,
):
    seq = lax.axis_index("seq")
    me = lax.axis_index("head")
    tokens, width = x_hbm.shape
    heads = d_ref.shape[1]
    blocks = tokens // BLOCK
    state = b_ref.shape[1]
    exact = groups * chunks * piece == width

    def behind(d):
        return lax.rem(me - d + groups, groups)

    def ahead(d):
        return lax.rem(me + d, groups)

    def column(group, k):
        return (group * chunks + k) * piece

    def clamped(start):
        return pl.multiple_of(start if exact else jnp.minimum(start, width - piece), LANES)

    def one_hot(start, count):
        row = lax.broadcasted_iota(jnp.int32, (count, piece), 0)
        col = lax.broadcasted_iota(jnp.int32, (count, piece), 1)
        low = row * head_dim - start
        hit = jnp.logical_and(col >= low, col < low + head_dim)
        return jnp.where(hit, 1.0, 0.0).astype(BF16)

    def x_copy(k, d):
        start = clamped(column(ahead(d), k))
        return pltpu.make_async_copy(x_hbm.at[:, pl.ds(start, piece)], x_s.at[k, d], x_sem.at[k, d])

    def out_copy(k, d):
        start = clamped(column(ahead(d), k))
        return pltpu.make_async_copy(out_s.at[k, d], out_hbm.at[:, pl.ds(start, piece)], o_sem.at[k, d])

    def m_copy(k, d):
        return pltpu.make_async_remote_copy(
            src_ref=ms_s.at[k, d], dst_ref=r_s.at[k, d], send_sem=ms_send.at[k, d],
            recv_sem=ms_recv.at[k, d], device_id=(seq, ahead(d)), device_id_type=MESH)

    def p_copy(k, d):
        return pltpu.make_async_remote_copy(
            src_ref=ps_s.at[k, d], dst_ref=pr_s.at[k, d], send_sem=ps_send.at[k, d],
            recv_sem=ps_recv.at[k, d], device_id=(seq, ahead(d)), device_id_type=MESH)

    def h_copy(k):
        return pltpu.make_async_remote_copy(
            src_ref=hout_s.at[k], dst_ref=hin_s.at[k], send_sem=h_send.at[k],
            recv_sem=h_recv.at[k], device_id=(lax.rem(seq + 1, shards), me), device_id_type=MESH)

    def t_copy(d):
        return pltpu.make_async_remote_copy(
            src_ref=tot_s, dst_ref=totr_s.at[d], send_sem=t_send.at[d],
            recv_sem=t_recv.at[d], device_id=(seq, ahead(d)), device_id_type=MESH)

    barrier = pltpu.get_barrier_semaphore()
    for d in range(1, groups):
        pl.semaphore_signal(barrier, inc=1, device_id=(seq, ahead(d)), device_id_type=MESH)
    for step in (1, shards - 1):
        pl.semaphore_signal(
            barrier, inc=1, device_id=(lax.rem(seq + step, shards), me), device_id_type=MESH)

    @pl.loop(0, chunks * groups)
    def _(p):
        k = p // groups
        x_copy(k, lax.rem(p - k * groups + 1, groups)).start()

    rows = lax.broadcasted_iota(jnp.int32, (BLOCK, BLOCK), 0)
    cols = lax.broadcasted_iota(jnp.int32, (BLOCK, BLOCK), 1)
    causal = rows >= cols
    lower = jnp.where(causal, 1.0, 0.0).astype(F32)
    middles, ends = [], []
    for b in range(blocks):
        at = pl.ds(b * BLOCK, BLOCK)
        running = jnp.dot(lower, d_ref[at, :], precision=PRECISE, preferred_element_type=F32)
        middle = running[BLOCK // 2 - 1:BLOCK // 2, :]
        middles.append(middle)
        ends.append(running[BLOCK - 1:BLOCK, :])
        gi_hi[at, :], gi_lo[at, :] = split2(jnp.exp(middle - running))
        gx_hi[at, :], gx_lo[at, :] = split2(jnp.exp(running - middle))
        c_block, b_block = c_ref[at, :], b_ref[at, :]
        scores = lax.dot_general(
            c_block, b_block, (((1,), (1,)), ((), ())), precision=PRECISE, preferred_element_type=F32)
        stacked = jnp.concatenate([jnp.where(causal, scores, 0.0), b_block.T], axis=0)
        l_hi[b], l_lo[b] = split2(stacked)
        cm_hi[b], cm_lo[b] = split2(c_block)
    total = sum(ends[1:], ends[0])
    tot_s[...] = jnp.zeros_like(tot_s)
    tot_s[0:1, 0:heads] = total
    totr_s[0] = jnp.zeros_like(tot_s)
    totr_s[0, 0:1, 0:heads] = total
    small = jnp.concatenate(
        [jnp.exp(m) for m in middles] + [jnp.exp(e - m) for e, m in zip(ends, middles)]
        + [jnp.exp(e) for e in ends] + [gain_ref[...]], axis=0)
    count = small.shape[0]
    row_a[0:count, :], row_b[0:count, :], row_c[0:count, :] = split3(small)

    pl.semaphore_wait(barrier, groups + 1)
    for d in range(1, groups):
        t_copy(d).start()

    @pl.loop(0, chunks * groups)
    def _(p):
        k = p // groups
        d = lax.rem(p - k * groups + 1, groups)
        hot = one_hot(column(ahead(d), k), heads)
        grow_in = dot(gi_hi[...], hot) + dot(gi_lo[...], hot)
        grow_out = dot(gx_hi[...], hot) + dot(gx_lo[...], hot)
        wide = dot(row_a[...], hot) + (dot(row_b[...], hot) + dot(row_c[...], hot))
        go_s[k, d] = grow_out
        rows_s[k, d] = wide[0:rows_s.shape[2]]
        gain = wide[3 * blocks:3 * blocks + 1]
        x_copy(k, d).wait()
        memory = None
        for b in range(blocks):
            low, high = b * BLOCK, (b + 1) * BLOCK
            x = x_s[k, d, low:high, :]
            both = dot3(l_hi[b], l_lo[b], x * grow_in[low:high])
            out_s[k, d, low:high, :] = both[:BLOCK] * grow_out[low:high] + gain * x
            added = both[BLOCK:] * wide[blocks + b:blocks + b + 1]
            if b > 0:
                m0_s[k, d, b - 1] = memory
                memory = memory * wide[2 * blocks + b:2 * blocks + b + 1] + added
            else:
                memory = added

        @pl.when(d == 0)
        def _():
            r_s[k, 0] = memory

        @pl.when(d != 0)
        def _():
            ms_s[k, d] = memory
            m_copy(k, d).start()

    for d in range(1, groups):
        t_copy(d).wait_recv()

    @pl.loop(0, chunks)
    def _(k):
        hot = one_hot(column(me, k), LANES)
        factors = []
        for j in range(groups):
            parts = split3(jnp.exp(totr_s[behind(j)]))
            factors.append((dot(parts[0], hot) + (dot(parts[1], hot) + dot(parts[2], hot)))[0:1])
        for d in range(1, groups):
            m_copy(k, d).wait_recv()
        running = r_s[k, behind(0)]
        decay = factors[0]
        bef_s[0] = jnp.zeros_like(running)
        a_s[0] = jnp.ones_like(a_s[0])
        for j in range(1, groups):
            bef_s[j] = running
            a_s[j] = jnp.broadcast_to(decay, a_s.shape[1:])
            running = factors[j] * running + r_s[k, behind(j)]
            decay = decay * factors[j]

        @pl.when(seq == 0)
        def _():
            hin_s[k] = jnp.zeros_like(running)

        @pl.when(seq > 0)
        def _():
            h_copy(k).wait_recv()

        incoming = hin_s[k]
        hout_s[k] = decay * incoming + running

        @pl.when(seq < shards - 1)
        def _():
            h_copy(k).start()

        for d in range(1, groups):
            j = ahead(d)
            ps_s[k, d] = a_s[j, 0:1] * incoming + bef_s[j]
            p_copy(k, d).start()
        pr_s[k, 0] = a_s[me, 0:1] * incoming + bef_s[me]

    @pl.loop(0, chunks * groups)
    def _(p):
        k = p // groups
        back = p - k * groups
        d = lax.rem(groups - back, groups)

        @pl.when(back != 0)
        def _():
            p_copy(k, back).wait_recv()

        arriving = pr_s[k, back]
        wide = rows_s[k, d]
        for b in range(blocks):
            low, high = b * BLOCK, (b + 1) * BLOCK
            if b > 0:
                so_far = wide[2 * blocks:2 * blocks + 1]
                for e in range(1, b):
                    so_far = so_far * wide[2 * blocks + e:2 * blocks + e + 1]
                entering = arriving * so_far + m0_s[k, d, b - 1]
            else:
                entering = arriving
            carried = dot3(cm_hi[b], cm_lo[b], entering * wide[b:b + 1])
            out_s[k, d, low:high, :] = out_s[k, d, low:high, :] + carried * go_s[k, d, low:high, :]
        if exact:
            out_copy(k, d).start()
        else:
            @pl.when(column(ahead(d), k) < width)
            def _():
                out_copy(k, d).start()

    for d in range(1, groups):
        t_copy(d).wait_send()

    @pl.loop(0, chunks)
    def _(k):
        @pl.when(seq < shards - 1)
        def _():
            h_copy(k).wait_send()

        for d in range(groups):
            if d > 0:
                m_copy(k, d).wait_send()
                p_copy(k, d).wait_send()
            if exact:
                out_copy(k, d).wait()
            else:
                @pl.when(column(ahead(d), k) < width)
                def _():
                    out_copy(k, d).wait()


def on_device(groups, shards, inputs, log_decay, input_map, output_map, skip_gain):
    tokens, width = inputs.shape
    heads = skip_gain.shape[0]
    state = input_map.shape[1]
    blocks = tokens // BLOCK
    chunks, piece = piece_plan(width, groups)
    row_count = -(-(3 * blocks + 1) // 16) * 16
    kept = -(-(3 * blocks + 1) // 8) * 8
    vmem = pltpu.VMEM
    dma = pltpu.SemaphoreType.DMA
    pieces = (chunks, groups)
    return pl.pallas_call(
        functools.partial(kernel, groups, shards, chunks, piece, width // heads),
        out_shape=jax.ShapeDtypeStruct((tokens, width), F32),
        in_specs=[pl.BlockSpec(memory_space=pl.ANY)] + [pl.BlockSpec(memory_space=vmem)] * 4,
        out_specs=pl.BlockSpec(memory_space=pl.ANY),
        scratch_shapes=[
            vmem(pieces + (tokens, piece), F32),
            vmem(pieces + (tokens, piece), F32),
            vmem(pieces + (tokens, piece), F32),
            vmem(pieces + (max(1, blocks - 1), state, piece), F32),
            vmem(pieces + (state, piece), F32),
            vmem(pieces + (state, piece), F32),
            vmem(pieces + (state, piece), F32),
            vmem(pieces + (state, piece), F32),
            vmem((chunks, state, piece), F32),
            vmem((chunks, state, piece), F32),
            vmem((groups, state, piece), F32),
            vmem((groups, 8, piece), F32),
            vmem(pieces + (kept, piece), F32),
            vmem((blocks, BLOCK + state, BLOCK), BF16),
            vmem((blocks, BLOCK + state, BLOCK), BF16),
            vmem((blocks, BLOCK, state), BF16),
            vmem((blocks, BLOCK, state), BF16),
            vmem((tokens, heads), BF16),
            vmem((tokens, heads), BF16),
            vmem((tokens, heads), BF16),
            vmem((tokens, heads), BF16),
            vmem((row_count, heads), BF16),
            vmem((row_count, heads), BF16),
            vmem((row_count, heads), BF16),
            vmem((8, LANES), F32),
            vmem((groups, 8, LANES), F32),
            dma(pieces), dma(pieces), dma(pieces), dma(pieces), dma(pieces), dma(pieces),
            dma((chunks,)), dma((chunks,)), dma((groups,)), dma((groups,)),
        ],
        compiler_params=pltpu.CompilerParams(
            collective_id=0, has_side_effects=True, vmem_limit_bytes=60 * 1024 * 1024),
    )(inputs, log_decay, input_map, output_map, skip_gain.reshape(1, heads))


def solution(mesh):
    rows = P(("seq", "head"), None)
    body = functools.partial(on_device, mesh.shape["head"], mesh.shape["seq"])
    return jax.shard_map(
        body, mesh=mesh, in_specs=(rows, rows, rows, rows, P()), out_specs=rows, check_vma=False
    )
```
